32 devices in a mesh: group: 2 (over x), dev: 16 (over z, y, core).
Axes of the slice: x: 2, y: 2, z: 4, core: 2. Of those that a mesh axis runs over, the one named last changes fastest.
Arguments:
- positions: float32 [256, 3, 544], P(('group', 'dev')), may hold values from -6 to 6
- analysis: float32 [289, 544], replicated, may hold values from -0.25 to 0.25
- synthesis: float32 [544, 289], replicated, may hold values from -0.375 to 0.375
- stiffness: float32 [289], replicated, may hold values from 0.1 to 10
- owner: int32 [1088, 1], P(('group', 'dev')), may hold values from 0 to 15; in each aligned block of 34 rows (0 to 33, 34 to 67, ...) at most 4 rows name the same one
- ulist: int32 [2048, 4], P(('group', 'dev')), may hold values from 0 to 191, as said below
Outputs:
- moved: float32 [256, 3, 544], P(('group', 'dev'))
- velocity: float32 [256, 3, 544], P(('group', 'dev'))
The draws below stay inside these ranges and needn't reach their ends.
Inputs may be any that keep to these rules, and one draw needn't show every extreme that they name: On the points of one device, no owner receives more than 4 blocks, and some owner receives exactly 4. `ulist`: entry 0 of row r is 64 + r % 64, the slot itself.
All inputs are finite; a program needn't handle non-finite values.
Results may differ from the reference program's by a relative error of at most 0.00011.
Values sent between devices are 32-bit elements; how exact they have to be, the bound alone decides.
A program may use at most 64 MiB of HBM per device.

```python
import math
import jax
import jax.numpy as jnp
import numpy as np
from jax import lax

P_SIZE = 544
NCOEF = 289
LEAF = 128
KNEAR = 4
STEPS = 1
C_DEV = 8
CELLS = 256
BLK_DEV = 34
NBLK = 1088
CAP = 4
SLOTS = 64
LIST_ROWS = 2048
N_GROUP = 2
N_DEV = 16


def draw_ulist(key, part):
    row_ids = jnp.arange(LIST_ROWS, dtype=jnp.int32)
    others = jax.random.randint(jax.random.fold_in(key, 11), (LIST_ROWS, KNEAR - 1), 0, 3 * SLOTS, dtype=jnp.int32)
    own_column = (SLOTS + row_ids % SLOTS)[:, None]
    listed = jnp.concatenate([own_column, others], axis=1)
    listed = listed.at[0, 1].set(0)
    listed = listed.at[LIST_ROWS - 1, KNEAR - 1].set(3 * SLOTS - 1)
    return listed.astype(jnp.int32)


def block_scale(key, shape, pieces, low, largest):
    gain, own = 1.0, jax.random.fold_in(key, 6)
    for dim, blocks in pieces:
        steps = jnp.exp(jax.random.uniform(jax.random.fold_in(own, dim), (blocks,), jnp.float32, low / len(pieces), largest / len(pieces)))
        gain = gain * jnp.repeat(steps, shape[dim] // blocks).reshape([-1 if axis == dim else 1 for axis in range(len(shape))])
    return gain


def shared_out(stream_key, own, number, rows, count, top, most, skew):
    ranking = jax.random.permutation(stream_key, count)
    packed, ordinary = shares(count, rows * top, most, skew, True), shares(count, rows * top, most, skew, False)
    places = jnp.arange(count)

    def named(tallies, turn):
        used = int((tallies > 0).sum())
        fixed = max(1, used // 4)
        shifted = fixed + (places - fixed + turn * (used - fixed)) % max(1, count - fixed)
        return jnp.zeros((count,), jnp.int32).at[ranking[jnp.where(places < fixed, places, shifted)]].set(jnp.asarray(tallies, jnp.int32))

    tallies = jnp.where(number % 4 == 0, named(packed, number // 4), named(ordinary, number - number // 4 - 1))
    mixed = jax.random.permutation(jax.random.fold_in(own, 3), count)
    giver, receiver = mixed[0:count // 2 * 2:2], mixed[1:count // 2 * 2:2]
    room = jnp.minimum(tallies[giver] - 1, most - tallies[receiver]) // 2
    room = jnp.where((giver == ranking[0]) | (receiver == ranking[0]) | (tallies[receiver] == 0), 0, jnp.maximum(room, 0))
    shifted = jax.random.randint(jax.random.fold_in(own, 4), (count // 2,), 0, 1 << 20) % (room + 1)
    tallies = tallies.at[giver].add(-shifted).at[receiver].add(shifted)
    items = jnp.searchsorted(jnp.cumsum(tallies), jnp.arange(rows * top), side="right").astype(jnp.int32)
    grid = items.reshape(top, rows).T
    grid = grid[jax.random.permutation(jax.random.fold_in(own, 1), rows)]
    turn = jax.random.randint(jax.random.fold_in(own, 2), (rows, 1), 0, top)
    return jnp.take_along_axis(grid, (jnp.arange(top)[None, :] + turn) % top, axis=1)


def shares(count, total, limit, lean, full):
    portions = [(1 << 20) // math.isqrt(standing ** lean) + 1 for standing in range(1, count + 1)]
    largest = limit if full else min(limit, max(-(-total // count), total * portions[0] // sum(portions)))
    least = 1 if total - largest >= count - 1 else 0
    counts, spare = [largest] + [least] * (count - 1), total - largest - least * (count - 1)
    while spare > 0:
        free = [i for i in range(1, count) if counts[i] < largest] or [i for i in range(1, count) if counts[i] < limit]
        pool, budget = sum([portions[i] for i in free]), spare
        for i in free:
            more = min(limit - counts[i], max(1, budget * portions[i] // pool), spare)
            counts[i] = counts[i] + more
            spare = spare - more
    return np.array(counts)


def normal_values(own_key, dims, spread, reach, cuts=(), kind=jnp.bfloat16):
    result = jax.random.normal(own_key, dims, jnp.float32) * spread
    if len(cuts) > 0:
        result = block_scale(own_key, dims, cuts, -0.22, 0.18) * result
    return jnp.clip(result, min=-reach, max=reach).astype(kind)


def setup_inputs(seed: int = 0) -> dict:
    splits = jax.random.split(jax.random.key(seed), 7)
    positions = normal_values(splits[0], (CELLS, 3, P_SIZE), 1.0, 6.0, ((0, 32),), jnp.float32)
    analysis = normal_values(splits[1], (NCOEF, P_SIZE), P_SIZE ** -0.5, 0.25, (), jnp.float32)
    synthesis = normal_values(splits[2], (P_SIZE, NCOEF), NCOEF ** -0.5, 0.375, (), jnp.float32)
    stiffness = jnp.clip(jnp.exp(jax.random.uniform(splits[3], (NCOEF,), jnp.float32, math.log(0.1), math.log(10.0))), 0.1, 10.0)
    owner_keys = jax.random.split(jax.random.fold_in(splits[4], 1), NBLK // BLK_DEV)
    owner_turns = jax.random.permutation(jax.random.fold_in(splits[4], 3), NBLK // BLK_DEV)
    owner = jax.vmap(lambda own, number: shared_out(jax.random.fold_in(splits[4], 2), own, number, BLK_DEV, N_DEV, 1, CAP, 2))(owner_keys, owner_turns).reshape((NBLK, 1))
    ulist = draw_ulist(jax.random.fold_in(splits[6], 71), 0)
    return {"positions": positions, "analysis": analysis, "synthesis": synthesis, "stiffness": stiffness, "owner": owner, "ulist": ulist}


SOFTENING = 0.25
KERNEL = 1.0 / (8.0 * math.pi)
TIME_STEP = 0.02
PRECISE = lax.Precision.HIGHEST

def spectral(shape_field, analysis, synthesis, weights):
    coeffs = jnp.einsum('ckp,mp->ckm', shape_field, analysis, precision=PRECISE)
    return jnp.einsum('ckm,pm->ckp', coeffs * weights, synthesis, precision=PRECISE)

def stokeslet(targets, sources):
    offset = targets[:, :, :, None] - sources[:, 0:3, None, :]
    forces = sources[:, 3:6, None, :]
    dist_sq = lax.optimization_barrier(jnp.sum(offset * offset, axis=1)) + SOFTENING
    kernel_scale = KERNEL / (dist_sq * jnp.sqrt(dist_sq))
    projected = lax.optimization_barrier(jnp.sum(offset * forces, axis=1))
    summed = ((dist_sq + SOFTENING) * kernel_scale)[:, None] * forces + (projected * kernel_scale)[:, None] * offset
    return lax.optimization_barrier(jnp.sum(summed, axis=3))

def reference(positions, analysis, synthesis, stiffness, owner, ulist):
    groups = N_GROUP
    dev_count = N_DEV
    device_count = groups * dev_count
    capacity = CAP
    slot_count = SLOTS
    block_count = device_count * BLK_DEV
    owner_dev = owner[:, 0].reshape(device_count, BLK_DEV)
    same_owner = owner_dev[:, :, None] == owner_dev[:, None, :]
    order_idx = jnp.arange(BLK_DEV, dtype=jnp.int32)
    earlier = order_idx[None, :] < order_idx[:, None]
    block_rank = lax.optimization_barrier(jnp.sum(jnp.where(same_owner & earlier[None], 1, 0), axis=2)).astype(jnp.int32)
    dev_all = jnp.arange(device_count, dtype=jnp.int32)
    group_of = dev_all // dev_count
    source_dev = dev_all % dev_count
    recv_dev = group_of[:, None] * dev_count + owner_dev
    recv_slot = source_dev[:, None] * capacity + block_rank
    flat_row = (recv_dev * slot_count + recv_slot).reshape(-1).astype(jnp.int32)
    slot_table = jnp.full((device_count * slot_count,), block_count, jnp.int32)
    slot_table = slot_table.at[flat_row].set(jnp.arange(block_count, dtype=jnp.int32))
    entries = ulist[flat_row]
    group_side = entries // slot_count
    slot_pos = entries % slot_count
    source_group = jnp.repeat(group_of, BLK_DEV)[:, None] + group_side - 1
    usable = (source_group >= 0) & (source_group < groups)
    owner_flat = owner_dev.reshape(-1)[:, None]
    lookup = ((jnp.clip(source_group, 0, groups - 1) * dev_count + owner_flat) * slot_count + slot_pos).astype(jnp.int32)
    source_ids = jnp.where(usable, slot_table[lookup], block_count).astype(jnp.int32)

    def to_blocks(values):
        shaped = values.reshape(device_count, C_DEV, 3, P_SIZE).transpose(0, 2, 1, 3)
        shaped = shaped.reshape(device_count, 3, BLK_DEV, LEAF).transpose(0, 2, 1, 3)
        return shaped.reshape(block_count, 3, LEAF)

    def from_blocks(values):
        shaped = values.reshape(device_count, BLK_DEV, 3, LEAF).transpose(0, 2, 1, 3)
        shaped = shaped.reshape(device_count, 3, C_DEV, P_SIZE).transpose(0, 2, 1, 3)
        return shaped.reshape(device_count * C_DEV, 3, P_SIZE)
    ones = jnp.ones((NCOEF,), jnp.float32)
    shape_field = positions
    velocity = jnp.zeros_like(positions)
    for time_step in range(STEPS):
        forces = -spectral(shape_field, analysis, synthesis, stiffness)
        payload = jnp.concatenate([to_blocks(shape_field), to_blocks(forces)], axis=1)
        payload = jnp.concatenate([payload, jnp.zeros((1, 6, LEAF), jnp.float32)], axis=0)

        def per_batch(block_ids):
            targets = payload[block_ids, 0:3]
            summed = jnp.zeros((block_ids.shape[0], 3, LEAF), jnp.float32)
            for entry in range(KNEAR):
                summed = summed + stokeslet(targets, payload[source_ids[block_ids, entry]])
            return summed
        flows = lax.map(per_batch, jnp.arange(block_count, dtype=jnp.int32).reshape(-1, 32))
        velocity = from_blocks(flows.reshape(block_count, 3, LEAF))
        shape_field = spectral(shape_field + TIME_STEP * velocity, analysis, synthesis, ones)
    return (shape_field, velocity)
```

```python
import math

import jax
import jax.numpy as jnp
from jax import lax
from jax.experimental import pallas as pl
from jax.experimental.pallas import tpu as pltpu
from jax.sharding import PartitionSpec as P

P_SIZE = 544
LEAF = 128
KNEAR = 4
C_DEV = 8
BLK_DEV = 34


SOFTENING = 0.25
KERNEL = 1.0 / (8.0 * math.pi)
TIME_STEP = 0.02
PRECISE = lax.Precision.HIGHEST


def with_halo(block, sides, width):
    for axis, dim in sides:
        count = lax.axis_size(axis)
        forward = [(i, i + 1) for i in range(count - 1)]
        backward = [(target, source) for source, target in forward]
        low = lax.ppermute(
            lax.slice_in_dim(block, block.shape[dim] - width, None, axis=dim), axis, forward
        )
        high = lax.ppermute(lax.slice_in_dim(block, 0, width, axis=dim), axis, backward)
        block = jnp.concatenate([low, block, high], axis=dim)
    return block


def split3(value):
    first = value.astype(jnp.bfloat16)
    rest = value - first.astype(jnp.float32)
    second = rest.astype(jnp.bfloat16)
    third = (rest - second.astype(jnp.float32)).astype(jnp.bfloat16)
    return first, second, third


def split2(value):
    first = value.astype(jnp.bfloat16)
    return first, (value - first.astype(jnp.float32)).astype(jnp.bfloat16)


def near_kernel(lists_ref, near_ref, flows_ref, table_ref):
    total = near_ref.shape[0]
    slot_count = flows_ref.shape[0]
    zeros4 = jnp.zeros((4, LEAF), jnp.float32)
    ones = jnp.ones((1, LEAF), jnp.float32)

    def prepare(slot, carry):
        data = near_ref[slot]
        y, f = data[0:3], data[3:6]
        y_sq = jnp.sum(y * y, axis=0, keepdims=True) + SOFTENING
        yf = -jnp.sum(y * f, axis=0, keepdims=True)
        dist = jnp.concatenate([-2.0 * y, y_sq, ones, jnp.zeros((3, LEAF), jnp.float32)], axis=0)
        proj = jnp.concatenate([f, yf, zeros4], axis=0)
        d1, d2, d3 = [piece.astype(jnp.float32) for piece in split3(dist)]
        p1, p2, p3 = [piece.astype(jnp.float32) for piece in split3(proj)]
        w_f = jnp.concatenate([f * KERNEL, jnp.zeros((5, LEAF), jnp.float32)], axis=0)
        w_y = jnp.concatenate([-KERNEL * y, KERNEL * ones, zeros4], axis=0)
        f1, f2 = [piece.astype(jnp.float32) for piece in split2(w_f)]
        y1, y2 = [piece.astype(jnp.float32) for piece in split2(w_y)]
        left = jnp.concatenate([d1, d2, d3, d1, d2, d1, f1, f2], axis=0)
        right = jnp.concatenate([p1, p2, p3, p1, p2, p1, y1, y2], axis=0)
        table_ref[slot, :, 0:LEAF] = left.astype(jnp.bfloat16)
        table_ref[slot, :, LEAF:] = right.astype(jnp.bfloat16)
        return carry

    lax.fori_loop(0, total, prepare, 0, unroll=4)
    own = slot_count

    def one_slot(slot, carry):
        x = near_ref[own + slot][0:3]
        x_sq = jnp.sum(x * x, axis=0, keepdims=True)
        base = jnp.concatenate([x, ones, x_sq, jnp.zeros((3, LEAF), jnp.float32)], axis=0)
        t1, t2, t3 = [piece.astype(jnp.float32) for piece in split3(base)]
        target = jnp.concatenate([t1, t1, t1, t2, t2, t3], axis=0).T.astype(jnp.bfloat16)
        total_c = None
        for entry in range(KNEAR):
            source = lists_ref[slot * KNEAR + entry]
            rows = table_ref[source]
            both = jnp.dot(target, rows[0:48], preferred_element_type=jnp.float32)
            rr, projected = both[:, 0:LEAF], both[:, LEAF:]
            inv = lax.rsqrt(rr)
            inv3 = inv * inv * inv
            a1, a2 = split2(inv + SOFTENING * inv3)
            b1, b2 = split2(projected * inv3)
            w_f, w_y = rows[48:64, 0:LEAF], rows[48:64, LEAF:]
            values = jnp.concatenate([a1, a2, b1, b2], axis=1)
            weights = jnp.concatenate([w_f, w_f, w_y, w_y], axis=1)
            part = lax.dot_general(
                values, weights, (((1,), (1,)), ((), ())), preferred_element_type=jnp.float32
            )
            total_c = part if total_c is None else total_c + part
        turned = total_c.T
        turned = turned[0:8] + turned[8:16]
        flows_ref[slot] = turned[0:3] + x * turned[3:4]
        return carry

    lax.fori_loop(0, slot_count, one_slot, 0, unroll=2)


def near_sum(near_data, lists):
    total = near_data.shape[0]
    slot_count = lists.shape[0]
    return pl.pallas_call(
        near_kernel,
        out_shape=jax.ShapeDtypeStruct((slot_count, 3, LEAF), jnp.float32),
        in_specs=[
            pl.BlockSpec(memory_space=pltpu.SMEM),
            pl.BlockSpec(memory_space=pltpu.VMEM),
        ],
        out_specs=pl.BlockSpec(memory_space=pltpu.VMEM),
        scratch_shapes=[pltpu.VMEM((total, 64, 2 * LEAF), jnp.bfloat16)],
    )(lists.reshape(-1), near_data)


def to_blocks(values):
    return values.transpose(1, 0, 2).reshape(3, BLK_DEV, LEAF).transpose(1, 0, 2)


def from_blocks(values):
    return values.transpose(1, 0, 2).reshape(3, C_DEV, P_SIZE).transpose(1, 0, 2)


def filtered(shape_field, analysis, synthesis):
    coeffs = jnp.einsum("ckp,mp->ckm", shape_field, analysis, precision=PRECISE)
    return jnp.einsum("ckm,pm->ckp", coeffs, synthesis, precision=PRECISE)


def shards(positions, analysis, synthesis, stiffness, owner, ulist):
    dev_count = lax.axis_size("dev")
    capacity = (BLK_DEV + dev_count - 1) // dev_count + 1
    slot_count = capacity * dev_count
    owner_dev = owner[:, 0]
    same_owner = owner_dev[:, None] == owner_dev[None, :]
    order_idx = jnp.arange(BLK_DEV, dtype=jnp.int32)
    earlier = order_idx[None, :] < order_idx[:, None]
    block_rank = jnp.sum(jnp.where(same_owner & earlier, 1, 0), axis=1).astype(jnp.int32)
    send_slot = owner_dev * capacity + block_rank
    onehot = (send_slot[:, None] == jnp.arange(slot_count, dtype=jnp.int32)[None, :]).astype(
        jnp.float32
    )
    shape_field = positions
    coeffs = jnp.einsum("ckp,mp->ckm", shape_field, analysis, precision=PRECISE)
    forces = -jnp.einsum("ckm,pm->ckp", coeffs * stiffness, synthesis, precision=PRECISE)
    payload = jnp.concatenate([to_blocks(shape_field), to_blocks(forces)], axis=1).reshape(
        BLK_DEV, 6 * LEAF
    )
    packed = jnp.dot(onehot.T, payload, precision=PRECISE).reshape(dev_count, capacity, 6 * LEAF)
    arrived = lax.all_to_all(packed, "dev", split_axis=0, concat_axis=0, tiled=True).reshape(
        slot_count, 6, LEAF
    )
    near_data = with_halo(arrived[None], (("group", 0),), 1)
    near_data = near_data.reshape(3 * slot_count, 6, LEAF)

    flows = near_sum(near_data, ulist)
    flows = flows.reshape(dev_count, capacity, 3 * LEAF)
    returned = lax.all_to_all(flows, "dev", split_axis=0, concat_axis=0, tiled=True).reshape(
        slot_count, 3 * LEAF
    )
    velocity = from_blocks(jnp.dot(onehot, returned, precision=PRECISE).reshape(BLK_DEV, 3, LEAF))
    shape_field = filtered(shape_field + TIME_STEP * velocity, analysis, synthesis)
    return (shape_field, velocity)


def solution(mesh):
    placed = (
        P(("group", "dev"), None, None),
        P(),
        P(),
        P(),
        P(("group", "dev"), None),
        P(("group", "dev"), None),
    )
    return jax.shard_map(
        shards,
        mesh=mesh,
        in_specs=placed,
        out_specs=(P(("group", "dev"), None, None), P(("group", "dev"), None, None)),
        check_vma=False,
    )
```

```python
import functools
import math

import jax
import jax.numpy as jnp
from jax import lax
from jax.experimental import pallas as pl
from jax.experimental.pallas import tpu as pltpu
from jax.sharding import PartitionSpec as P

P_SIZE = 544
LEAF = 128
KNEAR = 4
C_DEV = 8
ROWS = 16
BLK_DEV = 34


SOFTENING = 0.25
KERNEL = 1.0 / (8.0 * math.pi)
TIME_STEP = 0.02
PRECISE = lax.Precision.HIGHEST


def split3(value):
    first = value.astype(jnp.bfloat16)
    rest = value - first.astype(jnp.float32)
    second = rest.astype(jnp.bfloat16)
    third = (rest - second.astype(jnp.float32)).astype(jnp.bfloat16)
    return first, second, third


def split2(value):
    first = value.astype(jnp.bfloat16)
    return first, (value - first.astype(jnp.float32)).astype(jnp.bfloat16)


def near_kernel(lists_ref, near_ref, flows_ref, table_ref, dist0_ref, dist1_ref, value0_ref, value1_ref):
    total = near_ref.shape[0]
    slot_count = flows_ref.shape[0]
    zeros4 = jnp.zeros((4, LEAF), jnp.float32)
    ones = jnp.ones((1, LEAF), jnp.float32)

    def prepare(slot, carry):
        data = near_ref[slot]
        y, f = data[0:3], data[3:6]
        y_sq = jnp.sum(y * y, axis=0, keepdims=True) + SOFTENING
        yf = -jnp.sum(y * f, axis=0, keepdims=True)
        dist = jnp.concatenate([-2.0 * y, y_sq, ones, jnp.zeros((3, LEAF), jnp.float32)], axis=0)
        proj = jnp.concatenate([f, yf, zeros4], axis=0)
        d1, d2, d3 = [piece.astype(jnp.float32) for piece in split3(dist)]
        p1, p2, p3 = [piece.astype(jnp.float32) for piece in split3(proj)]
        w_f = jnp.concatenate([f * KERNEL, jnp.zeros((5, LEAF), jnp.float32)], axis=0)
        w_y = jnp.concatenate([-KERNEL * y, KERNEL * ones, zeros4], axis=0)
        f1, f2 = [piece.astype(jnp.float32) for piece in split2(w_f)]
        y1, y2 = [piece.astype(jnp.float32) for piece in split2(w_y)]
        left = jnp.concatenate([d1, d2, d3, d1, d2, d1, f1, f2], axis=0)
        right = jnp.concatenate([p1, p2, p3, p1, p2, p1, y1, y2], axis=0)
        table_ref[slot, :, 0:LEAF] = left.astype(jnp.bfloat16)
        table_ref[slot, :, LEAF:] = right.astype(jnp.bfloat16)
        return carry

    lax.fori_loop(0, total, prepare, 0, unroll=4)
    own = slot_count

    def distances(slot, out_ref):
        x = near_ref[own + slot][0:3]
        x_sq = jnp.sum(x * x, axis=0, keepdims=True)
        base = jnp.concatenate([x, ones, x_sq, jnp.zeros((3, LEAF), jnp.float32)], axis=0)
        t1, t2, t3 = [piece.astype(jnp.float32) for piece in split3(base)]
        target = jnp.concatenate([t1, t1, t1, t2, t2, t3], axis=0).T.astype(jnp.bfloat16)
        for entry in range(KNEAR):
            source = lists_ref[slot * KNEAR + entry]
            out_ref[entry] = jnp.dot(
                target, table_ref[source, 0:48], preferred_element_type=jnp.float32
            )

    def kernels(in_ref, out_ref):
        for entry in range(KNEAR):
            for row in range(0, LEAF, ROWS):
                rr = in_ref[entry, row : row + ROWS, 0:LEAF]
                projected = in_ref[entry, row : row + ROWS, LEAF:]
                inv = lax.rsqrt(rr)
                inv3 = inv * inv * inv
                parts = split2(inv + SOFTENING * inv3) + split2(projected * inv3)
                for piece in range(4):
                    start = (entry * 4 + piece) * LEAF
                    out_ref[row : row + ROWS, start : start + LEAF] = parts[piece]

    def sums(slot, in_ref):
        weights = []
        for entry in range(KNEAR):
            source = lists_ref[slot * KNEAR + entry]
            w_f = table_ref[source, 48:64, 0:LEAF]
            w_y = table_ref[source, 48:64, LEAF:]
            weights += [w_f, w_f, w_y, w_y]
        total_c = lax.dot_general(
            in_ref[...],
            jnp.concatenate(weights, axis=1),
            (((1,), (1,)), ((), ())),
            preferred_element_type=jnp.float32,
        )
        turned = total_c.T
        turned = turned[0:8] + turned[8:16]
        x = near_ref[own + slot][0:3]
        flows_ref[slot] = turned[0:3] + x * turned[3:4]

    dist = (dist0_ref, dist1_ref)
    value = (value0_ref, value1_ref)
    distances(0, dist0_ref)
    value1_ref[...] = jnp.zeros_like(value1_ref)

    def pair(step, carry):
        for parity in range(2):
            slot = 2 * step + parity
            distances(jnp.minimum(slot + 1, slot_count - 1), dist[1 - parity])
            kernels(dist[parity], value[parity])
            sums(jnp.maximum(slot - 1, 0), value[1 - parity])
        return carry

    lax.fori_loop(0, slot_count // 2, pair, 0)
    sums(slot_count - 1, value1_ref)


def near_sum(near_data, lists):
    total = near_data.shape[0]
    slot_count = lists.shape[0]
    return pl.pallas_call(
        near_kernel,
        out_shape=jax.ShapeDtypeStruct((slot_count, 3, LEAF), jnp.float32),
        in_specs=[
            pl.BlockSpec(memory_space=pltpu.SMEM),
            pl.BlockSpec(memory_space=pltpu.VMEM),
        ],
        out_specs=pl.BlockSpec(memory_space=pltpu.VMEM),
        scratch_shapes=[
            pltpu.VMEM((total, 64, 2 * LEAF), jnp.bfloat16),
            pltpu.VMEM((KNEAR, LEAF, 2 * LEAF), jnp.float32),
            pltpu.VMEM((KNEAR, LEAF, 2 * LEAF), jnp.float32),
            pltpu.VMEM((LEAF, 4 * KNEAR * LEAF), jnp.bfloat16),
            pltpu.VMEM((LEAF, 4 * KNEAR * LEAF), jnp.bfloat16),
        ],
    )(lists.reshape(-1), near_data)


MESH = pl.DeviceIdType.MESH


def beside(group, groups, action):
    pl.when(group + 1 < groups)(functools.partial(action, 0, group + 1))
    pl.when(group > 0)(functools.partial(action, 1, group - 1))


def greet(count, me, groups=None, group=None):
    barrier = pltpu.get_barrier_semaphore()

    def signal(step, carry):
        pl.semaphore_signal(
            barrier, inc=1, device_id={"dev": lax.rem(me + step, count)}, device_id_type=MESH
        )
        return carry

    lax.fori_loop(1, count, signal, 0)
    if groups is not None:

        def signal_beside(way, other):
            pl.semaphore_signal(barrier, inc=1, device_id={"group": other}, device_id_type=MESH)

        beside(group, groups, signal_beside)
        sides = jnp.minimum(group, 1) + jnp.minimum(groups - 1 - group, 1)
        pl.semaphore_wait(barrier, count - 1 + sides)
    else:
        pl.semaphore_wait(barrier, count - 1)


def forward_kernel(packed_ref, near_ref, own_sem, send_sem, recv_sem, side_send, side_recv):
    count, groups = lax.axis_size("dev"), lax.axis_size("group")
    me, group = lax.axis_index("dev"), lax.axis_index("group")
    greet(count, me, groups, group)
    own = pltpu.make_async_copy(packed_ref.at[me], near_ref.at[1, me], own_sem)
    own.start()

    def across(step):
        peer = lax.rem(me + step, count)
        return pltpu.make_async_remote_copy(
            src_ref=packed_ref.at[peer],
            dst_ref=near_ref.at[1, me],
            send_sem=send_sem.at[step],
            recv_sem=recv_sem.at[step],
            device_id={"dev": peer},
            device_id_type=MESH,
        )

    def along(step, way, other):
        chunk = lax.rem(me - step + count, count)
        return pltpu.make_async_remote_copy(
            src_ref=near_ref.at[1, chunk],
            dst_ref=near_ref.at[2 * way, chunk],
            send_sem=side_send.at[way, step],
            recv_sem=side_recv.at[way, step],
            device_id={"group": other},
            device_id_type=MESH,
        )

    def start(step, carry):
        across(step).start()
        return carry

    lax.fori_loop(1, count, start, 0)

    def clear(side):
        near_ref[side] = jnp.zeros_like(near_ref[side])

    pl.when(group == 0)(lambda: clear(0))
    pl.when(group == groups - 1)(lambda: clear(2))
    own.wait()
    beside(group, groups, lambda way, other: along(0, way, other).start())

    def relay(step, carry):
        across(step).wait_recv()
        beside(group, groups, lambda way, other: along(step, way, other).start())
        return carry

    lax.fori_loop(1, count, relay, 0)

    def finish(step, carry):
        pl.when(group + 1 < groups)(lambda: along(step, 0, group + 1).wait_send())
        pl.when(group > 0)(lambda: along(step, 1, group - 1).wait_send())
        pl.when(group > 0)(lambda: along(step, 0, group - 1).wait_recv())
        pl.when(group + 1 < groups)(lambda: along(step, 1, group + 1).wait_recv())
        return carry

    lax.fori_loop(0, count, finish, 0)

    def sent(step, carry):
        across(step).wait_send()
        return carry

    lax.fori_loop(1, count, sent, 0)


def forward(packed):
    count = packed.shape[0]
    sem = pltpu.SemaphoreType.DMA
    return pl.pallas_call(
        forward_kernel,
        out_shape=jax.ShapeDtypeStruct((3,) + packed.shape, packed.dtype),
        in_specs=[pl.BlockSpec(memory_space=pltpu.VMEM)],
        out_specs=pl.BlockSpec(memory_space=pltpu.VMEM),
        scratch_shapes=[sem, sem((count,)), sem((count,)), sem((2, count)), sem((2, count))],
        compiler_params=pltpu.CompilerParams(collective_id=0, has_side_effects=True),
    )(packed)


def back_kernel(flows_ref, back_ref, own_sem, send_sem, recv_sem):
    count, me = lax.axis_size("dev"), lax.axis_index("dev")
    greet(count, me)
    own = pltpu.make_async_copy(flows_ref.at[me], back_ref.at[me], own_sem)
    own.start()

    def across(step):
        peer = lax.rem(me + step, count)
        return pltpu.make_async_remote_copy(
            src_ref=flows_ref.at[peer],
            dst_ref=back_ref.at[me],
            send_sem=send_sem.at[step],
            recv_sem=recv_sem.at[step],
            device_id={"dev": peer},
            device_id_type=MESH,
        )

    def start(step, carry):
        across(step).start()
        return carry

    def finish(step, carry):
        across(step).wait()
        return carry

    lax.fori_loop(1, count, start, 0)
    own.wait()
    lax.fori_loop(1, count, finish, 0)


def back(flows):
    count = flows.shape[0]
    sem = pltpu.SemaphoreType.DMA
    return pl.pallas_call(
        back_kernel,
        out_shape=jax.ShapeDtypeStruct(flows.shape, flows.dtype),
        in_specs=[pl.BlockSpec(memory_space=pltpu.VMEM)],
        out_specs=pl.BlockSpec(memory_space=pltpu.VMEM),
        scratch_shapes=[sem, sem((count,)), sem((count,))],
        compiler_params=pltpu.CompilerParams(collective_id=1, has_side_effects=True),
    )(flows)


def to_blocks(values):
    return values.transpose(1, 0, 2).reshape(3, BLK_DEV, LEAF).transpose(1, 0, 2)


def from_blocks(values):
    return values.transpose(1, 0, 2).reshape(3, C_DEV, P_SIZE).transpose(1, 0, 2)


def filtered(shape_field, analysis, synthesis):
    coeffs = jnp.einsum("ckp,mp->ckm", shape_field, analysis, precision=PRECISE)
    return jnp.einsum("ckm,pm->ckp", coeffs, synthesis, precision=PRECISE)


def shards(positions, analysis, synthesis, stiffness, owner, ulist):
    dev_count = lax.axis_size("dev")
    capacity = (BLK_DEV + dev_count - 1) // dev_count + 1
    slot_count = capacity * dev_count
    owner_dev = owner[:, 0]
    same_owner = owner_dev[:, None] == owner_dev[None, :]
    order_idx = jnp.arange(BLK_DEV, dtype=jnp.int32)
    earlier = order_idx[None, :] < order_idx[:, None]
    block_rank = jnp.sum(jnp.where(same_owner & earlier, 1, 0), axis=1).astype(jnp.int32)
    send_slot = owner_dev * capacity + block_rank
    onehot = (send_slot[:, None] == jnp.arange(slot_count, dtype=jnp.int32)[None, :]).astype(
        jnp.float32
    )
    shape_field = positions
    coeffs = jnp.einsum("ckp,mp->ckm", shape_field, analysis, precision=PRECISE)
    forces = -jnp.einsum("ckm,pm->ckp", coeffs * stiffness, synthesis, precision=PRECISE)
    payload = jnp.concatenate([to_blocks(shape_field), to_blocks(forces)], axis=1).reshape(
        BLK_DEV, 6 * LEAF
    )
    packed = jnp.dot(onehot.T, payload, precision=PRECISE).reshape(dev_count, capacity, 6, LEAF)
    near_data = forward(packed).reshape(3 * slot_count, 6, LEAF)
    flows = near_sum(near_data, ulist).reshape(dev_count, capacity, 3, LEAF)
    returned = back(flows).reshape(slot_count, 3 * LEAF)
    velocity = from_blocks(jnp.dot(onehot, returned, precision=PRECISE).reshape(BLK_DEV, 3, LEAF))
    shape_field = filtered(shape_field + TIME_STEP * velocity, analysis, synthesis)
    return (shape_field, velocity)


def solution(mesh):
    placed = (
        P(("group", "dev"), None, None),
        P(),
        P(),
        P(),
        P(("group", "dev"), None),
        P(("group", "dev"), None),
    )
    return jax.shard_map(
        shards,
        mesh=mesh,
        in_specs=placed,
        out_specs=(P(("group", "dev"), None, None), P(("group", "dev"), None, None)),
        check_vma=False,
    )
```

```python
import functools
import math

import jax
import jax.numpy as jnp
from jax import lax
from jax.experimental import pallas as pl
from jax.experimental.pallas import tpu as pltpu
from jax.sharding import PartitionSpec as P

P_SIZE = 544
LEAF = 128
KNEAR = 4
C_DEV = 8
ROWS = 16
WIDTH = 4
BLK_DEV = 34


SOFTENING = 0.25
KERNEL = 1.0 / (8.0 * math.pi)
TIME_STEP = 0.02
PRECISE = lax.Precision.HIGHEST


def split3(value):
    first = value.astype(jnp.bfloat16)
    rest = value - first.astype(jnp.float32)
    second = rest.astype(jnp.bfloat16)
    third = (rest - second.astype(jnp.float32)).astype(jnp.bfloat16)
    return first, second, third


def split2(value):
    first = value.astype(jnp.bfloat16)
    return first, (value - first.astype(jnp.float32)).astype(jnp.bfloat16)


def near_kernel(
    lists_ref, near_ref, flows_ref, table_ref, target_ref, total_ref,
    dist0_ref, dist1_ref, value0_ref, value1_ref, item_slot, item_source,
):
    slot_count = flows_ref.shape[0]
    zeros4 = jnp.zeros((4, LEAF), jnp.float32)
    ones = jnp.ones((1, LEAF), jnp.float32)
    low, high = lists_ref[slot_count * KNEAR], lists_ref[slot_count * KNEAR + 1]

    def prepare(slot):
        data = near_ref[slot]
        y, f = data[0:3], data[3:6]
        y_sq = jnp.sum(y * y, axis=0, keepdims=True)
        yf = -jnp.sum(y * f, axis=0, keepdims=True)
        dist = jnp.concatenate(
            [-2.0 * y, y_sq + SOFTENING, ones, jnp.zeros((3, LEAF), jnp.float32)], axis=0
        )
        proj = jnp.concatenate([f, yf, zeros4], axis=0)
        d1, d2, d3 = [piece.astype(jnp.float32) for piece in split3(dist)]
        p1, p2, p3 = [piece.astype(jnp.float32) for piece in split3(proj)]
        w_f = jnp.concatenate([f * KERNEL, jnp.zeros((5, LEAF), jnp.float32)], axis=0)
        w_y = jnp.concatenate([-KERNEL * y, KERNEL * ones, zeros4], axis=0)
        f1, f2 = [piece.astype(jnp.float32) for piece in split2(w_f)]
        y1, y2 = [piece.astype(jnp.float32) for piece in split2(w_y)]
        left = jnp.concatenate([d1, d2, d3, d1, d2, d1, f1, f2], axis=0)
        right = jnp.concatenate([p1, p2, p3, p1, p2, p1, y1, y2], axis=0)
        table_ref[slot, :, 0:LEAF] = left.astype(jnp.bfloat16)
        table_ref[slot, :, LEAF:] = right.astype(jnp.bfloat16)
        return y, y_sq

    def own_slot(slot, count):
        x, x_sq = prepare(slot_count + slot)
        base = jnp.concatenate([x, ones, x_sq, jnp.zeros((3, LEAF), jnp.float32)], axis=0)
        t1, t2, t3 = [piece.astype(jnp.float32) for piece in split3(base)]
        target = jnp.concatenate([t1, t1, t1, t2, t2, t3], axis=0)
        target_ref[slot] = target.T.astype(jnp.bfloat16)
        total_ref[slot] = jnp.zeros((8, LEAF), jnp.float32)
        for entry in range(KNEAR):
            source = lists_ref[slot * KNEAR + entry]
            item_slot[count] = slot
            item_source[count] = source
            count = count + jnp.where((source >= low) & (source < high), 1, 0)
        return count

    def four(step, carry):
        for place in range(4):
            prepare(4 * step + place)
        return carry

    count = lax.fori_loop(0, slot_count, own_slot, 0, unroll=4)
    lax.fori_loop(low // 4, slot_count // 4, four, 0)
    lax.fori_loop(slot_count // 2, high // 4, four, 0)
    target_ref[slot_count] = target_ref[0]
    total_ref[slot_count] = jnp.zeros((8, LEAF), jnp.float32)
    for extra in range(2 * WIDTH):
        item_slot[count + extra] = slot_count
        item_source[count + extra] = slot_count

    def distances(group, out_ref):
        for place in range(WIDTH):
            item = group * WIDTH + place
            out_ref[place] = jnp.dot(
                target_ref[item_slot[item]],
                table_ref[item_source[item], 0:48],
                preferred_element_type=jnp.float32,
            )

    def kernels(in_ref, out_ref):
        for place in range(WIDTH):
            for row in range(0, LEAF, ROWS):
                rr = in_ref[place, row : row + ROWS, 0:LEAF]
                projected = in_ref[place, row : row + ROWS, LEAF:]
                inv = lax.rsqrt(rr)
                inv3 = inv * inv * inv
                parts = split2(inv + SOFTENING * inv3) + split2(projected * inv3)
                for piece in range(4):
                    start = piece * LEAF
                    out_ref[place, row : row + ROWS, start : start + LEAF] = parts[piece]

    def sums(group, in_ref):
        for place in range(WIDTH):
            item = group * WIDTH + place
            source = item_source[item]
            w_f = table_ref[source, 48:64, 0:LEAF]
            w_y = table_ref[source, 48:64, LEAF:]
            part = lax.dot_general(
                jnp.concatenate([w_f, w_f, w_y, w_y], axis=1),
                in_ref[place],
                (((1,), (1,)), ((), ())),
                preferred_element_type=jnp.float32,
            )
            total_ref[item_slot[item]] += part[0:8] + part[8:16]

    dist = (dist0_ref, dist1_ref)
    value = (value0_ref, value1_ref)
    distances(0, dist0_ref)
    value1_ref[...] = jnp.zeros_like(value1_ref)
    pairs = (count + 2 * WIDTH - 1) // (2 * WIDTH)

    def pair(step, carry):
        for parity in range(2):
            group = 2 * step + parity
            distances(jnp.minimum(group + 1, 2 * pairs - 1), dist[1 - parity])
            kernels(dist[parity], value[parity])
            sums(jnp.maximum(group - 1, 0), value[1 - parity])
        return carry

    lax.fori_loop(0, pairs, pair, 0)
    sums(2 * pairs - 1, value1_ref)

    def finish(slot, carry):
        turned = total_ref[slot]
        flows_ref[slot] = turned[0:3] + near_ref[slot_count + slot][0:3] * turned[3:4]
        return carry

    lax.fori_loop(0, slot_count, finish, 0, unroll=8)


def near_sum(near_data, lists):
    total = near_data.shape[0]
    slot_count = lists.shape[0]
    group, groups = lax.axis_index("group"), lax.axis_size("group")
    low = jnp.where(group == 0, slot_count, 0)
    high = jnp.where(group == groups - 1, 2 * slot_count, 3 * slot_count)
    items = slot_count * KNEAR + 4 * WIDTH
    return pl.pallas_call(
        near_kernel,
        out_shape=jax.ShapeDtypeStruct((slot_count, 3, LEAF), jnp.float32),
        in_specs=[
            pl.BlockSpec(memory_space=pltpu.SMEM),
            pl.BlockSpec(memory_space=pltpu.VMEM),
        ],
        out_specs=pl.BlockSpec(memory_space=pltpu.VMEM),
        scratch_shapes=[
            pltpu.VMEM((total, 64, 2 * LEAF), jnp.bfloat16),
            pltpu.VMEM((slot_count + 1, LEAF, 48), jnp.bfloat16),
            pltpu.VMEM((slot_count + 1, 8, LEAF), jnp.float32),
            pltpu.VMEM((WIDTH, LEAF, 2 * LEAF), jnp.float32),
            pltpu.VMEM((WIDTH, LEAF, 2 * LEAF), jnp.float32),
            pltpu.VMEM((WIDTH, LEAF, 4 * LEAF), jnp.bfloat16),
            pltpu.VMEM((WIDTH, LEAF, 4 * LEAF), jnp.bfloat16),
            pltpu.SMEM((items,), jnp.int32),
            pltpu.SMEM((items,), jnp.int32),
        ],
    )(jnp.concatenate([lists.reshape(-1), jnp.stack([low, high])]), near_data)


MESH = pl.DeviceIdType.MESH


def beside(group, groups, action):
    pl.when(group + 1 < groups)(functools.partial(action, 0, group + 1))
    pl.when(group > 0)(functools.partial(action, 1, group - 1))


def greet(count, me, groups=None, group=None):
    barrier = pltpu.get_barrier_semaphore()

    def signal(step, carry):
        pl.semaphore_signal(
            barrier, inc=1, device_id={"dev": lax.rem(me + step, count)}, device_id_type=MESH
        )
        return carry

    lax.fori_loop(1, count, signal, 0)
    if groups is not None:

        def signal_beside(way, other):
            pl.semaphore_signal(barrier, inc=1, device_id={"group": other}, device_id_type=MESH)

        beside(group, groups, signal_beside)
        sides = jnp.minimum(group, 1) + jnp.minimum(groups - 1 - group, 1)
        pl.semaphore_wait(barrier, count - 1 + sides)
    else:
        pl.semaphore_wait(barrier, count - 1)


def forward_kernel(packed_ref, near_ref, own_sem, send_sem, recv_sem, side_send, side_recv):
    count, groups = lax.axis_size("dev"), lax.axis_size("group")
    me, group = lax.axis_index("dev"), lax.axis_index("group")
    greet(count, me, groups, group)
    own = pltpu.make_async_copy(packed_ref.at[me], near_ref.at[1, me], own_sem)
    own.start()

    def across(step):
        peer = lax.rem(me + step, count)
        return pltpu.make_async_remote_copy(
            src_ref=packed_ref.at[peer],
            dst_ref=near_ref.at[1, me],
            send_sem=send_sem.at[step],
            recv_sem=recv_sem.at[step],
            device_id={"dev": peer},
            device_id_type=MESH,
        )

    def along(step, way, other):
        chunk = lax.rem(me - step + count, count)
        return pltpu.make_async_remote_copy(
            src_ref=near_ref.at[1, chunk],
            dst_ref=near_ref.at[2 * way, chunk],
            send_sem=side_send.at[way, step],
            recv_sem=side_recv.at[way, step],
            device_id={"group": other},
            device_id_type=MESH,
        )

    def start(step, carry):
        across(step).start()
        return carry

    lax.fori_loop(1, count, start, 0)

    def clear(side):
        near_ref[side] = jnp.zeros_like(near_ref[side])

    pl.when(group == 0)(lambda: clear(0))
    pl.when(group == groups - 1)(lambda: clear(2))
    own.wait()
    beside(group, groups, lambda way, other: along(0, way, other).start())

    def relay(step, carry):
        across(step).wait_recv()
        beside(group, groups, lambda way, other: along(step, way, other).start())
        return carry

    lax.fori_loop(1, count, relay, 0)

    def finish(step, carry):
        pl.when(group + 1 < groups)(lambda: along(step, 0, group + 1).wait_send())
        pl.when(group > 0)(lambda: along(step, 1, group - 1).wait_send())
        pl.when(group > 0)(lambda: along(step, 0, group - 1).wait_recv())
        pl.when(group + 1 < groups)(lambda: along(step, 1, group + 1).wait_recv())
        return carry

    lax.fori_loop(0, count, finish, 0)

    def sent(step, carry):
        across(step).wait_send()
        return carry

    lax.fori_loop(1, count, sent, 0)


def forward(packed):
    count = packed.shape[0]
    sem = pltpu.SemaphoreType.DMA
    return pl.pallas_call(
        forward_kernel,
        out_shape=jax.ShapeDtypeStruct((3,) + packed.shape, packed.dtype),
        in_specs=[pl.BlockSpec(memory_space=pltpu.VMEM)],
        out_specs=pl.BlockSpec(memory_space=pltpu.VMEM),
        scratch_shapes=[sem, sem((count,)), sem((count,)), sem((2, count)), sem((2, count))],
        compiler_params=pltpu.CompilerParams(collective_id=0, has_side_effects=True),
    )(packed)


def back_kernel(flows_ref, back_ref, own_sem, send_sem, recv_sem):
    count, me = lax.axis_size("dev"), lax.axis_index("dev")
    greet(count, me)
    own = pltpu.make_async_copy(flows_ref.at[me], back_ref.at[me], own_sem)
    own.start()

    def across(step):
        peer = lax.rem(me + step, count)
        return pltpu.make_async_remote_copy(
            src_ref=flows_ref.at[peer],
            dst_ref=back_ref.at[me],
            send_sem=send_sem.at[step],
            recv_sem=recv_sem.at[step],
            device_id={"dev": peer},
            device_id_type=MESH,
        )

    def start(step, carry):
        across(step).start()
        return carry

    def finish(step, carry):
        across(step).wait()
        return carry

    lax.fori_loop(1, count, start, 0)
    own.wait()
    lax.fori_loop(1, count, finish, 0)


def back(flows):
    count = flows.shape[0]
    sem = pltpu.SemaphoreType.DMA
    return pl.pallas_call(
        back_kernel,
        out_shape=jax.ShapeDtypeStruct(flows.shape, flows.dtype),
        in_specs=[pl.BlockSpec(memory_space=pltpu.VMEM)],
        out_specs=pl.BlockSpec(memory_space=pltpu.VMEM),
        scratch_shapes=[sem, sem((count,)), sem((count,))],
        compiler_params=pltpu.CompilerParams(collective_id=1, has_side_effects=True),
    )(flows)


def to_blocks(values):
    return values.transpose(1, 0, 2).reshape(3, BLK_DEV, LEAF).transpose(1, 0, 2)


def from_blocks(values):
    return values.transpose(1, 0, 2).reshape(3, C_DEV, P_SIZE).transpose(1, 0, 2)


def filtered(shape_field, analysis, synthesis):
    coeffs = jnp.einsum("ckp,mp->ckm", shape_field, analysis, precision=PRECISE)
    return jnp.einsum("ckm,pm->ckp", coeffs, synthesis, precision=PRECISE)


def shards(positions, analysis, synthesis, stiffness, owner, ulist):
    dev_count = lax.axis_size("dev")
    capacity = (BLK_DEV + dev_count - 1) // dev_count + 1
    slot_count = capacity * dev_count
    owner_dev = owner[:, 0]
    same_owner = owner_dev[:, None] == owner_dev[None, :]
    order_idx = jnp.arange(BLK_DEV, dtype=jnp.int32)
    earlier = order_idx[None, :] < order_idx[:, None]
    block_rank = jnp.sum(jnp.where(same_owner & earlier, 1, 0), axis=1).astype(jnp.int32)
    send_slot = owner_dev * capacity + block_rank
    onehot = (send_slot[:, None] == jnp.arange(slot_count, dtype=jnp.int32)[None, :]).astype(
        jnp.float32
    )
    shape_field = positions
    coeffs = jnp.einsum("ckp,mp->ckm", shape_field, analysis, precision=PRECISE)
    forces = -jnp.einsum("ckm,pm->ckp", coeffs * stiffness, synthesis, precision=PRECISE)
    payload = jnp.concatenate([to_blocks(shape_field), to_blocks(forces)], axis=1).reshape(
        BLK_DEV, 6 * LEAF
    )
    packed = jnp.dot(onehot.T, payload, precision=PRECISE).reshape(dev_count, capacity, 6, LEAF)
    near_data = forward(packed).reshape(3 * slot_count, 6, LEAF)
    flows = near_sum(near_data, ulist).reshape(dev_count, capacity, 3, LEAF)
    returned = back(flows).reshape(slot_count, 3 * LEAF)
    velocity = from_blocks(jnp.dot(onehot, returned, precision=PRECISE).reshape(BLK_DEV, 3, LEAF))
    shape_field = filtered(shape_field + TIME_STEP * velocity, analysis, synthesis)
    return (shape_field, velocity)


def solution(mesh):
    placed = (
        P(("group", "dev"), None, None),
        P(),
        P(),
        P(),
        P(("group", "dev"), None),
        P(("group", "dev"), None),
    )
    return jax.shard_map(
        shards,
        mesh=mesh,
        in_specs=placed,
        out_specs=(P(("group", "dev"), None, None), P(("group", "dev"), None, None)),
        check_vma=False,
    )
```

```python
import functools
import math

import jax
import jax.numpy as jnp
from jax import lax
from jax.experimental import pallas as pl
from jax.experimental.pallas import tpu as pltpu
from jax.sharding import PartitionSpec as P

P_SIZE = 544
LEAF = 128
KNEAR = 4
C_DEV = 8
ROWS = 16
WIDTH = 4
BLK_DEV = 34


SOFTENING = 0.25
KERNEL = 1.0 / (8.0 * math.pi)
TIME_STEP = 0.02
PRECISE = lax.Precision.HIGHEST


def split3(value):
    first = value.astype(jnp.bfloat16)
    rest = value - first.astype(jnp.float32)
    second = rest.astype(jnp.bfloat16)
    third = (rest - second.astype(jnp.float32)).astype(jnp.bfloat16)
    return first, second, third


def split2(value):
    first = value.astype(jnp.bfloat16)
    return first, (value - first.astype(jnp.float32)).astype(jnp.bfloat16)


def near_kernel(
    lists_ref, near_ref, flows_ref, table_ref, target_ref, total_ref,
    dist0_ref, dist1_ref, value0_ref, value1_ref, item_slot, item_source,
):
    slot_count = flows_ref.shape[0]
    zeros4 = jnp.zeros((4, LEAF), jnp.float32)
    ones = jnp.ones((1, LEAF), jnp.float32)
    group, groups = lax.axis_index("group"), lax.axis_size("group")
    low = jnp.where(group == 0, slot_count, 0)
    high = jnp.where(group == groups - 1, 2 * slot_count, 3 * slot_count)

    def prepare(slot):
        data = near_ref[slot]
        y, f = data[0:3], data[3:6]
        y_sq = jnp.sum(y * y, axis=0, keepdims=True)
        yf = -jnp.sum(y * f, axis=0, keepdims=True)
        dist = jnp.concatenate(
            [-2.0 * y, y_sq + SOFTENING, ones, jnp.zeros((3, LEAF), jnp.float32)], axis=0
        )
        proj = jnp.concatenate([f, yf, zeros4], axis=0)
        d1, d2, d3 = [piece.astype(jnp.float32) for piece in split3(dist)]
        p1, p2, p3 = [piece.astype(jnp.float32) for piece in split3(proj)]
        w_f = jnp.concatenate([f * KERNEL, jnp.zeros((5, LEAF), jnp.float32)], axis=0)
        w_y = jnp.concatenate([-KERNEL * y, KERNEL * ones, zeros4], axis=0)
        f1, f2 = [piece.astype(jnp.float32) for piece in split2(w_f)]
        y1, y2 = [piece.astype(jnp.float32) for piece in split2(w_y)]
        left = jnp.concatenate([d1, d2, d3, d1, d2, d1, f1, f2], axis=0)
        right = jnp.concatenate([p1, p2, p3, p1, p2, p1, y1, y2], axis=0)
        table_ref[slot, :, 0:LEAF] = left.astype(jnp.bfloat16)
        table_ref[slot, :, LEAF:] = right.astype(jnp.bfloat16)
        return y, y_sq

    def own_slot(slot, count):
        x, x_sq = prepare(slot_count + slot)
        base = jnp.concatenate([x, ones, x_sq, jnp.zeros((3, LEAF), jnp.float32)], axis=0)
        t1, t2, t3 = [piece.astype(jnp.float32) for piece in split3(base)]
        target = jnp.concatenate([t1, t1, t1, t2, t2, t3], axis=0)
        target_ref[slot] = target.T.astype(jnp.bfloat16)
        total_ref[slot] = jnp.zeros((8, LEAF), jnp.float32)
        for entry in range(KNEAR):
            source = lists_ref[entry, slot]
            item_slot[count] = slot
            item_source[count] = source
            count = count + jnp.where((source >= low) & (source < high), 1, 0)
        return count

    def four(step, carry):
        for place in range(4):
            prepare(4 * step + place)
        return carry

    count = lax.fori_loop(0, slot_count, own_slot, 0, unroll=4)
    lax.fori_loop(low // 4, slot_count // 4, four, 0)
    lax.fori_loop(slot_count // 2, high // 4, four, 0)
    target_ref[slot_count] = target_ref[0]
    total_ref[slot_count] = jnp.zeros((8, LEAF), jnp.float32)
    for extra in range(2 * WIDTH):
        item_slot[count + extra] = slot_count
        item_source[count + extra] = slot_count

    def distances(group, out_ref):
        for place in range(WIDTH):
            item = group * WIDTH + place
            out_ref[place] = jnp.dot(
                target_ref[item_slot[item]],
                table_ref[item_source[item], 0:48],
                preferred_element_type=jnp.float32,
            )

    def kernels(in_ref, out_ref):
        for place in range(WIDTH):
            for row in range(0, LEAF, ROWS):
                rr = in_ref[place, row : row + ROWS, 0:LEAF]
                projected = in_ref[place, row : row + ROWS, LEAF:]
                inv = lax.rsqrt(rr)
                inv3 = inv * inv * inv
                parts = split2(inv + SOFTENING * inv3) + split2(projected * inv3)
                for piece in range(4):
                    start = piece * LEAF
                    out_ref[place, row : row + ROWS, start : start + LEAF] = parts[piece]

    def sums(group, in_ref):
        for place in range(WIDTH):
            item = group * WIDTH + place
            source = item_source[item]
            w_f = table_ref[source, 48:64, 0:LEAF]
            w_y = table_ref[source, 48:64, LEAF:]
            part = lax.dot_general(
                jnp.concatenate([w_f, w_f, w_y, w_y], axis=1),
                in_ref[place],
                (((1,), (1,)), ((), ())),
                preferred_element_type=jnp.float32,
            )
            total_ref[item_slot[item]] += part[0:8] + part[8:16]

    dist = (dist0_ref, dist1_ref)
    value = (value0_ref, value1_ref)
    distances(0, dist0_ref)
    value1_ref[...] = jnp.zeros_like(value1_ref)
    pairs = (count + 2 * WIDTH - 1) // (2 * WIDTH)

    def pair(step, carry):
        for parity in range(2):
            group = 2 * step + parity
            distances(jnp.minimum(group + 1, 2 * pairs - 1), dist[1 - parity])
            kernels(dist[parity], value[parity])
            sums(jnp.maximum(group - 1, 0), value[1 - parity])
        return carry

    lax.fori_loop(0, pairs, pair, 0)
    sums(2 * pairs - 1, value1_ref)

    def finish(slot, carry):
        turned = total_ref[slot]
        flows_ref[slot] = turned[0:3] + near_ref[slot_count + slot][0:3] * turned[3:4]
        return carry

    lax.fori_loop(0, slot_count, finish, 0, unroll=8)


def near_sum(near_data, lists):
    total = near_data.shape[0]
    slot_count = lists.shape[0]
    items = slot_count * KNEAR + 4 * WIDTH
    return pl.pallas_call(
        near_kernel,
        out_shape=jax.ShapeDtypeStruct((slot_count, 3, LEAF), jnp.float32),
        in_specs=[
            pl.BlockSpec(memory_space=pltpu.SMEM),
            pl.BlockSpec(memory_space=pltpu.VMEM),
        ],
        out_specs=pl.BlockSpec(memory_space=pltpu.VMEM),
        scratch_shapes=[
            pltpu.VMEM((total, 64, 2 * LEAF), jnp.bfloat16),
            pltpu.VMEM((slot_count + 1, LEAF, 48), jnp.bfloat16),
            pltpu.VMEM((slot_count + 1, 8, LEAF), jnp.float32),
            pltpu.VMEM((WIDTH, LEAF, 2 * LEAF), jnp.float32),
            pltpu.VMEM((WIDTH, LEAF, 2 * LEAF), jnp.float32),
            pltpu.VMEM((WIDTH, LEAF, 4 * LEAF), jnp.bfloat16),
            pltpu.VMEM((WIDTH, LEAF, 4 * LEAF), jnp.bfloat16),
            pltpu.SMEM((items,), jnp.int32),
            pltpu.SMEM((items,), jnp.int32),
        ],
        compiler_params=pltpu.CompilerParams(),
    )(lists.T, near_data)


MESH = pl.DeviceIdType.MESH


def beside(group, groups, action):
    pl.when(group + 1 < groups)(functools.partial(action, 0, group + 1))
    pl.when(group > 0)(functools.partial(action, 1, group - 1))


def greet(count, me, groups=None, group=None):
    barrier = pltpu.get_barrier_semaphore()

    def signal(step, carry):
        pl.semaphore_signal(
            barrier, inc=1, device_id={"dev": lax.rem(me + step, count)}, device_id_type=MESH
        )
        return carry

    lax.fori_loop(1, count, signal, 0)
    if groups is not None:

        def signal_beside(way, other):
            pl.semaphore_signal(barrier, inc=1, device_id={"group": other}, device_id_type=MESH)

        beside(group, groups, signal_beside)
        sides = jnp.minimum(group, 1) + jnp.minimum(groups - 1 - group, 1)
        pl.semaphore_wait(barrier, count - 1 + sides)
    else:
        pl.semaphore_wait(barrier, count - 1)


def forward_kernel(packed_ref, near_ref, own_sem, send_sem, recv_sem, side_send, side_recv):
    count, groups = lax.axis_size("dev"), lax.axis_size("group")
    me, group = lax.axis_index("dev"), lax.axis_index("group")
    greet(count, me, groups, group)
    own = pltpu.make_async_copy(packed_ref.at[me], near_ref.at[1, me], own_sem)
    own.start()

    def across(step):
        peer = lax.rem(me + step, count)
        return pltpu.make_async_remote_copy(
            src_ref=packed_ref.at[peer],
            dst_ref=near_ref.at[1, me],
            send_sem=send_sem.at[step],
            recv_sem=recv_sem.at[step],
            device_id={"dev": peer},
            device_id_type=MESH,
        )

    def along(step, way, other):
        chunk = lax.rem(me - step + count, count)
        return pltpu.make_async_remote_copy(
            src_ref=near_ref.at[1, chunk],
            dst_ref=near_ref.at[2 * way, chunk],
            send_sem=side_send.at[way, step],
            recv_sem=side_recv.at[way, step],
            device_id={"group": other},
            device_id_type=MESH,
        )

    def start(step, carry):
        across(step).start()
        return carry

    lax.fori_loop(1, count, start, 0)

    def clear(side):
        near_ref[side] = jnp.zeros_like(near_ref[side])

    pl.when(group == 0)(lambda: clear(0))
    pl.when(group == groups - 1)(lambda: clear(2))
    own.wait()
    beside(group, groups, lambda way, other: along(0, way, other).start())

    def relay(step, carry):
        across(step).wait_recv()
        beside(group, groups, lambda way, other: along(step, way, other).start())
        return carry

    lax.fori_loop(1, count, relay, 0)

    def finish(step, carry):
        pl.when(group + 1 < groups)(lambda: along(step, 0, group + 1).wait_send())
        pl.when(group > 0)(lambda: along(step, 1, group - 1).wait_send())
        pl.when(group > 0)(lambda: along(step, 0, group - 1).wait_recv())
        pl.when(group + 1 < groups)(lambda: along(step, 1, group + 1).wait_recv())
        return carry

    lax.fori_loop(0, count, finish, 0)

    def sent(step, carry):
        across(step).wait_send()
        return carry

    lax.fori_loop(1, count, sent, 0)


def forward(packed):
    count = packed.shape[0]
    sem = pltpu.SemaphoreType.DMA
    return pl.pallas_call(
        forward_kernel,
        out_shape=jax.ShapeDtypeStruct((3,) + packed.shape, packed.dtype),
        in_specs=[pl.BlockSpec(memory_space=pltpu.VMEM)],
        out_specs=pl.BlockSpec(memory_space=pltpu.VMEM),
        scratch_shapes=[sem, sem((count,)), sem((count,)), sem((2, count)), sem((2, count))],
        compiler_params=pltpu.CompilerParams(collective_id=0, has_side_effects=True),
    )(packed)


def back_kernel(flows_ref, back_ref, own_sem, send_sem, recv_sem):
    count, me = lax.axis_size("dev"), lax.axis_index("dev")
    greet(count, me)
    own = pltpu.make_async_copy(flows_ref.at[me], back_ref.at[me], own_sem)
    own.start()

    def across(step):
        peer = lax.rem(me + step, count)
        return pltpu.make_async_remote_copy(
            src_ref=flows_ref.at[peer],
            dst_ref=back_ref.at[me],
            send_sem=send_sem.at[step],
            recv_sem=recv_sem.at[step],
            device_id={"dev": peer},
            device_id_type=MESH,
        )

    def start(step, carry):
        across(step).start()
        return carry

    def finish(step, carry):
        across(step).wait()
        return carry

    lax.fori_loop(1, count, start, 0)
    own.wait()
    lax.fori_loop(1, count, finish, 0)


def back(flows):
    count = flows.shape[0]
    sem = pltpu.SemaphoreType.DMA
    return pl.pallas_call(
        back_kernel,
        out_shape=jax.ShapeDtypeStruct(flows.shape, flows.dtype),
        in_specs=[pl.BlockSpec(memory_space=pltpu.VMEM)],
        out_specs=pl.BlockSpec(memory_space=pltpu.VMEM),
        scratch_shapes=[sem, sem((count,)), sem((count,))],
        compiler_params=pltpu.CompilerParams(collective_id=1, has_side_effects=True),
    )(flows)


def to_blocks(values):
    return values.transpose(1, 0, 2).reshape(3, BLK_DEV, LEAF).transpose(1, 0, 2)


def from_blocks(values):
    return values.transpose(1, 0, 2).reshape(3, C_DEV, P_SIZE).transpose(1, 0, 2)


def filtered(shape_field, analysis, synthesis):
    coeffs = jnp.einsum("ckp,mp->ckm", shape_field, analysis, precision=PRECISE)
    return jnp.einsum("ckm,pm->ckp", coeffs, synthesis, precision=PRECISE)


def shards(positions, analysis, synthesis, stiffness, owner, ulist):
    dev_count = lax.axis_size("dev")
    capacity = (BLK_DEV + dev_count - 1) // dev_count + 1
    slot_count = capacity * dev_count
    owner_dev = owner[:, 0]
    same_owner = owner_dev[:, None] == owner_dev[None, :]
    order_idx = jnp.arange(BLK_DEV, dtype=jnp.int32)
    earlier = order_idx[None, :] < order_idx[:, None]
    block_rank = jnp.sum(jnp.where(same_owner & earlier, 1, 0), axis=1).astype(jnp.int32)
    send_slot = owner_dev * capacity + block_rank
    onehot = (send_slot[:, None] == jnp.arange(slot_count, dtype=jnp.int32)[None, :]).astype(
        jnp.float32
    )
    shape_field = positions
    coeffs = jnp.einsum("ckp,mp->ckm", shape_field, analysis, precision=PRECISE)
    forces = -jnp.einsum("ckm,pm->ckp", coeffs * stiffness, synthesis, precision=PRECISE)
    payload = jnp.concatenate([to_blocks(shape_field), to_blocks(forces)], axis=1).reshape(
        BLK_DEV, 6 * LEAF
    )
    packed = jnp.dot(onehot.T, payload, precision=PRECISE).reshape(dev_count, capacity, 6, LEAF)
    near_data = forward(packed).reshape(3 * slot_count, 6, LEAF)
    flows = near_sum(near_data, ulist).reshape(dev_count, capacity, 3, LEAF)
    returned = back(flows).reshape(slot_count, 3 * LEAF)
    velocity = from_blocks(jnp.dot(onehot, returned, precision=PRECISE).reshape(BLK_DEV, 3, LEAF))
    shape_field = filtered(shape_field + TIME_STEP * velocity, analysis, synthesis)
    return (shape_field, velocity)


def solution(mesh):
    placed = (
        P(("group", "dev"), None, None),
        P(),
        P(),
        P(),
        P(("group", "dev"), None),
        P(("group", "dev"), None),
    )
    return jax.shard_map(
        shards,
        mesh=mesh,
        in_specs=placed,
        out_specs=(P(("group", "dev"), None, None), P(("group", "dev"), None, None)),
        check_vma=False,
    )
```

```python
import functools
import math

import jax
import jax.numpy as jnp
from jax import lax
from jax.experimental import pallas as pl
from jax.experimental.pallas import tpu as pltpu
from jax.sharding import PartitionSpec as P

P_SIZE = 544
LEAF = 128
KNEAR = 4
C_DEV = 8
ROWS = 16
WIDTH = 4
BLK_DEV = 34


SOFTENING = 0.25
KERNEL = 1.0 / (8.0 * math.pi)
TIME_STEP = 0.02
PRECISE = lax.Precision.HIGHEST


def split3(value):
    first = value.astype(jnp.bfloat16)
    rest = value - first.astype(jnp.float32)
    second = rest.astype(jnp.bfloat16)
    third = (rest - second.astype(jnp.float32)).astype(jnp.bfloat16)
    return first, second, third


def split2(value):
    first = value.astype(jnp.bfloat16)
    return first, (value - first.astype(jnp.float32)).astype(jnp.bfloat16)


def near_kernel(
    lists_ref, near_ref, flows_ref, table_ref, target_ref, total_ref,
    dist0_ref, dist1_ref, value0_ref, value1_ref, item_slot, item_source,
):
    slot_count = flows_ref.shape[0]
    zeros4 = jnp.zeros((4, LEAF), jnp.float32)
    ones = jnp.ones((1, LEAF), jnp.float32)
    group, groups = lax.axis_index("group"), lax.axis_size("group")
    low = jnp.where(group == 0, slot_count, 0)
    high = jnp.where(group == groups - 1, 2 * slot_count, 3 * slot_count)

    def prepare(slot):
        data = near_ref[slot]
        y, f = data[0:3], data[3:6]
        y_sq = jnp.sum(y * y, axis=0, keepdims=True)
        yf = -jnp.sum(y * f, axis=0, keepdims=True)
        dist = jnp.concatenate(
            [-2.0 * y, y_sq + SOFTENING, ones, jnp.zeros((3, LEAF), jnp.float32)], axis=0
        )
        proj = jnp.concatenate([f, yf, zeros4], axis=0)
        d1, d2, d3 = [piece.astype(jnp.float32) for piece in split3(dist)]
        p1, p2, p3 = [piece.astype(jnp.float32) for piece in split3(proj)]
        w_f = jnp.concatenate([f * KERNEL, jnp.zeros((5, LEAF), jnp.float32)], axis=0)
        w_y = jnp.concatenate([-KERNEL * y, KERNEL * ones, zeros4], axis=0)
        f1, f2 = [piece.astype(jnp.float32) for piece in split2(w_f)]
        y1, y2 = [piece.astype(jnp.float32) for piece in split2(w_y)]
        left = jnp.concatenate([d1, d2, d3, d1, d2, d1, f1, f2], axis=0)
        right = jnp.concatenate([p1, p2, p3, p1, p2, p1, y1, y2], axis=0)
        table_ref[slot, :, 0:LEAF] = left.astype(jnp.bfloat16)
        table_ref[slot, :, LEAF:] = right.astype(jnp.bfloat16)
        return y, y_sq

    def own_slot(slot, count):
        x, x_sq = prepare(slot_count + slot)
        base = jnp.concatenate([x, ones, x_sq, jnp.zeros((3, LEAF), jnp.float32)], axis=0)
        t1, t2, t3 = [piece.astype(jnp.float32) for piece in split3(base)]
        target = jnp.concatenate([t1, t1, t1, t2, t2, t3], axis=0)
        target_ref[slot] = target.T.astype(jnp.bfloat16)
        total_ref[slot] = jnp.zeros((8, LEAF), jnp.float32)
        for entry in range(KNEAR):
            source = lists_ref[entry, slot]
            item_slot[count] = slot
            item_source[count] = source
            count = count + jnp.where((source >= low) & (source < high), 1, 0)
        return count

    def four(step, carry):
        for place in range(4):
            prepare(4 * step + place)
        return carry

    count = lax.fori_loop(0, slot_count, own_slot, 0, unroll=16)
    lax.fori_loop(low // 4, slot_count // 4, four, 0)
    lax.fori_loop(slot_count // 2, high // 4, four, 0)
    target_ref[slot_count] = target_ref[0]
    total_ref[slot_count] = jnp.zeros((8, LEAF), jnp.float32)
    for extra in range(2 * WIDTH):
        item_slot[count + extra] = slot_count
        item_source[count + extra] = slot_count

    def distances(group, out_ref):
        for place in range(WIDTH):
            item = group * WIDTH + place
            out_ref[place] = jnp.dot(
                target_ref[item_slot[item]],
                table_ref[item_source[item], 0:48],
                preferred_element_type=jnp.float32,
            )

    def kernels(in_ref, out_ref):
        for place in range(WIDTH):
            for row in range(0, LEAF, ROWS):
                rr = in_ref[place, row : row + ROWS, 0:LEAF]
                projected = in_ref[place, row : row + ROWS, LEAF:]
                inv = lax.rsqrt(rr)
                inv3 = inv * inv * inv
                parts = split2(inv + SOFTENING * inv3) + split2(projected * inv3)
                for piece in range(4):
                    start = piece * LEAF
                    out_ref[place, row : row + ROWS, start : start + LEAF] = parts[piece]

    def sums(group, in_ref):
        for place in range(WIDTH):
            item = group * WIDTH + place
            source = item_source[item]
            w_f = table_ref[source, 48:64, 0:LEAF]
            w_y = table_ref[source, 48:64, LEAF:]
            part = lax.dot_general(
                jnp.concatenate([w_f, w_f, w_y, w_y], axis=1),
                in_ref[place],
                (((1,), (1,)), ((), ())),
                preferred_element_type=jnp.float32,
            )
            total_ref[item_slot[item]] += part[0:8] + part[8:16]

    dist = (dist0_ref, dist1_ref)
    value = (value0_ref, value1_ref)
    distances(0, dist0_ref)
    value1_ref[...] = jnp.zeros_like(value1_ref)
    pairs = (count + 2 * WIDTH - 1) // (2 * WIDTH)

    def pair(step, carry):
        for parity in range(2):
            group = 2 * step + parity
            distances(jnp.minimum(group + 1, 2 * pairs - 1), dist[1 - parity])
            kernels(dist[parity], value[parity])
            sums(jnp.maximum(group - 1, 0), value[1 - parity])
        return carry

    lax.fori_loop(0, pairs, pair, 0)
    sums(2 * pairs - 1, value1_ref)

    def finish(slot, carry):
        turned = total_ref[slot]
        flows_ref[slot] = turned[0:3] + near_ref[slot_count + slot][0:3] * turned[3:4]
        return carry

    lax.fori_loop(0, slot_count, finish, 0, unroll=8)


def near_sum(near_data, lists):
    total = near_data.shape[0]
    slot_count = lists.shape[0]
    items = slot_count * KNEAR + 4 * WIDTH
    return pl.pallas_call(
        near_kernel,
        out_shape=jax.ShapeDtypeStruct((slot_count, 3, LEAF), jnp.float32),
        in_specs=[
            pl.BlockSpec(memory_space=pltpu.SMEM),
            pl.BlockSpec(memory_space=pltpu.VMEM),
        ],
        out_specs=pl.BlockSpec(memory_space=pltpu.VMEM),
        scratch_shapes=[
            pltpu.VMEM((total, 64, 2 * LEAF), jnp.bfloat16),
            pltpu.VMEM((slot_count + 1, LEAF, 48), jnp.bfloat16),
            pltpu.VMEM((slot_count + 1, 8, LEAF), jnp.float32),
            pltpu.VMEM((WIDTH, LEAF, 2 * LEAF), jnp.float32),
            pltpu.VMEM((WIDTH, LEAF, 2 * LEAF), jnp.float32),
            pltpu.VMEM((WIDTH, LEAF, 4 * LEAF), jnp.bfloat16),
            pltpu.VMEM((WIDTH, LEAF, 4 * LEAF), jnp.bfloat16),
            pltpu.SMEM((items,), jnp.int32),
            pltpu.SMEM((items,), jnp.int32),
        ],
        compiler_params=pltpu.CompilerParams(),
    )(lists.T, near_data)


MESH = pl.DeviceIdType.MESH


def beside(group, groups, action):
    pl.when(group + 1 < groups)(functools.partial(action, 0, group + 1))
    pl.when(group > 0)(functools.partial(action, 1, group - 1))


def greet(count, me, groups=None, group=None):
    barrier = pltpu.get_barrier_semaphore()

    def signal(step, carry):
        pl.semaphore_signal(
            barrier, inc=1, device_id={"dev": lax.rem(me + step, count)}, device_id_type=MESH
        )
        return carry

    lax.fori_loop(1, count, signal, 0)
    if groups is not None:

        def signal_beside(way, other):
            pl.semaphore_signal(barrier, inc=1, device_id={"group": other}, device_id_type=MESH)

        beside(group, groups, signal_beside)
        sides = jnp.minimum(group, 1) + jnp.minimum(groups - 1 - group, 1)
        pl.semaphore_wait(barrier, count - 1 + sides)
    else:
        pl.semaphore_wait(barrier, count - 1)


def forward_kernel(packed_ref, near_ref, own_sem, send_sem, recv_sem, side_send, side_recv):
    count, groups = lax.axis_size("dev"), lax.axis_size("group")
    me, group = lax.axis_index("dev"), lax.axis_index("group")
    greet(count, me, groups, group)
    own = pltpu.make_async_copy(packed_ref.at[me], near_ref.at[1, me], own_sem)
    own.start()

    def across(step):
        peer = lax.rem(me + step, count)
        return pltpu.make_async_remote_copy(
            src_ref=packed_ref.at[peer],
            dst_ref=near_ref.at[1, me],
            send_sem=send_sem.at[step],
            recv_sem=recv_sem.at[step],
            device_id={"dev": peer},
            device_id_type=MESH,
        )

    def along(step, way, other):
        chunk = lax.rem(me - step + count, count)
        return pltpu.make_async_remote_copy(
            src_ref=near_ref.at[1, chunk],
            dst_ref=near_ref.at[2 * way, chunk],
            send_sem=side_send.at[way, step],
            recv_sem=side_recv.at[way, step],
            device_id={"group": other},
            device_id_type=MESH,
        )

    def start(step, carry):
        across(step).start()
        return carry

    lax.fori_loop(1, count, start, 0)

    def clear(side):
        near_ref[side] = jnp.zeros_like(near_ref[side])

    pl.when(group == 0)(lambda: clear(0))
    pl.when(group == groups - 1)(lambda: clear(2))
    own.wait()
    beside(group, groups, lambda way, other: along(0, way, other).start())

    def relay(step, carry):
        across(step).wait_recv()
        beside(group, groups, lambda way, other: along(step, way, other).start())
        return carry

    lax.fori_loop(1, count, relay, 0)

    def finish(step, carry):
        pl.when(group + 1 < groups)(lambda: along(step, 0, group + 1).wait_send())
        pl.when(group > 0)(lambda: along(step, 1, group - 1).wait_send())
        pl.when(group > 0)(lambda: along(step, 0, group - 1).wait_recv())
        pl.when(group + 1 < groups)(lambda: along(step, 1, group + 1).wait_recv())
        return carry

    lax.fori_loop(0, count, finish, 0)

    def sent(step, carry):
        across(step).wait_send()
        return carry

    lax.fori_loop(1, count, sent, 0)


def forward(packed):
    count = packed.shape[0]
    sem = pltpu.SemaphoreType.DMA
    return pl.pallas_call(
        forward_kernel,
        out_shape=jax.ShapeDtypeStruct((3,) + packed.shape, packed.dtype),
        in_specs=[pl.BlockSpec(memory_space=pltpu.VMEM)],
        out_specs=pl.BlockSpec(memory_space=pltpu.VMEM),
        scratch_shapes=[sem, sem((count,)), sem((count,)), sem((2, count)), sem((2, count))],
        compiler_params=pltpu.CompilerParams(collective_id=0, has_side_effects=True),
    )(packed)


def back_kernel(flows_ref, back_ref, own_sem, send_sem, recv_sem):
    count, me = lax.axis_size("dev"), lax.axis_index("dev")
    greet(count, me)
    own = pltpu.make_async_copy(flows_ref.at[me], back_ref.at[me], own_sem)
    own.start()

    def across(step):
        peer = lax.rem(me + step, count)
        return pltpu.make_async_remote_copy(
            src_ref=flows_ref.at[peer],
            dst_ref=back_ref.at[me],
            send_sem=send_sem.at[step],
            recv_sem=recv_sem.at[step],
            device_id={"dev": peer},
            device_id_type=MESH,
        )

    def start(step, carry):
        across(step).start()
        return carry

    def finish(step, carry):
        across(step).wait()
        return carry

    lax.fori_loop(1, count, start, 0)
    own.wait()
    lax.fori_loop(1, count, finish, 0)


def back(flows):
    count = flows.shape[0]
    sem = pltpu.SemaphoreType.DMA
    return pl.pallas_call(
        back_kernel,
        out_shape=jax.ShapeDtypeStruct(flows.shape, flows.dtype),
        in_specs=[pl.BlockSpec(memory_space=pltpu.VMEM)],
        out_specs=pl.BlockSpec(memory_space=pltpu.VMEM),
        scratch_shapes=[sem, sem((count,)), sem((count,))],
        compiler_params=pltpu.CompilerParams(collective_id=1, has_side_effects=True),
    )(flows)


def to_blocks(values):
    return values.transpose(1, 0, 2).reshape(3, BLK_DEV, LEAF).transpose(1, 0, 2)


def from_blocks(values):
    return values.transpose(1, 0, 2).reshape(3, C_DEV, P_SIZE).transpose(1, 0, 2)


def filtered(shape_field, analysis, synthesis):
    coeffs = jnp.einsum("ckp,mp->ckm", shape_field, analysis, precision=PRECISE)
    return jnp.einsum("ckm,pm->ckp", coeffs, synthesis, precision=PRECISE)


def shards(positions, analysis, synthesis, stiffness, owner, ulist):
    dev_count = lax.axis_size("dev")
    capacity = (BLK_DEV + dev_count - 1) // dev_count + 1
    slot_count = capacity * dev_count
    owner_dev = owner[:, 0]
    same_owner = owner_dev[:, None] == owner_dev[None, :]
    order_idx = jnp.arange(BLK_DEV, dtype=jnp.int32)
    earlier = order_idx[None, :] < order_idx[:, None]
    block_rank = jnp.sum(jnp.where(same_owner & earlier, 1, 0), axis=1).astype(jnp.int32)
    send_slot = owner_dev * capacity + block_rank
    onehot = (send_slot[:, None] == jnp.arange(slot_count, dtype=jnp.int32)[None, :]).astype(
        jnp.float32
    )
    shape_field = positions
    coeffs = jnp.einsum("ckp,mp->ckm", shape_field, analysis, precision=PRECISE)
    forces = -jnp.einsum("ckm,pm->ckp", coeffs * stiffness, synthesis, precision=PRECISE)
    payload = jnp.concatenate([to_blocks(shape_field), to_blocks(forces)], axis=1).reshape(
        BLK_DEV, 6 * LEAF
    )
    packed = jnp.dot(onehot.T, payload, precision=PRECISE).reshape(dev_count, capacity, 6, LEAF)
    near_data = forward(packed).reshape(3 * slot_count, 6, LEAF)
    flows = near_sum(near_data, ulist).reshape(dev_count, capacity, 3, LEAF)
    returned = back(flows).reshape(slot_count, 3 * LEAF)
    velocity = from_blocks(jnp.dot(onehot, returned, precision=PRECISE).reshape(BLK_DEV, 3, LEAF))
    shape_field = filtered(shape_field + TIME_STEP * velocity, analysis, synthesis)
    return (shape_field, velocity)


def solution(mesh):
    placed = (
        P(("group", "dev"), None, None),
        P(),
        P(),
        P(),
        P(("group", "dev"), None),
        P(("group", "dev"), None),
    )
    return jax.shard_map(
        shards,
        mesh=mesh,
        in_specs=placed,
        out_specs=(P(("group", "dev"), None, None), P(("group", "dev"), None, None)),
        check_vma=False,
    )
```
